32 devices in a mesh: row: 8 (over z, x), col: 4 (over y, core).
Axes of the slice: x: 2, y: 2, z: 4, core: 2. Of those that a mesh axis runs over, the one named last changes fastest.
Arguments:
- start_vector: float32 [12288, 12288], P('row', 'col'), may hold values from -6 to 6, as said below
- ham_blocks: bfloat16 [384, 128, 128], P('row'), may hold values from -0.1875 to 0.1875
- diagonal: float32 [12288], replicated, may hold values from -1 to 1
- pair_lists: int32 [3, 8, 64], replicated, may hold values from 0 to 47, as said below
- pair_counts: int32 [8], replicated, may hold values from 16 to 64, as said below
- hot_blocks: int32 [8, 2], replicated, may hold values from 0 to 11, as said below
- selection: int32 [8, 8], replicated, may hold values from 0 to 1
Outputs:
- first_iterate: float32 [12288, 12288], P('row', 'col')
- second_iterate: float32 [12288, 12288], P('row', 'col')
The draws below stay inside these ranges and needn't reach their ends.
Inputs may be any that keep to these rules, and one draw needn't show every extreme that they name: start_vector is symmetric: entry (a, b) equals entry (b, a). `pair_lists`: component 0 is a tile (0 to 7), component 1 a block of a tile (0 to 11), component 2 a block id (0 to 47); slot k < 8 of every list has source tile k. `pair_counts`: some tile has all 64 slots live. `hot_blocks`: the 2 blocks of a tile are distinct.
All inputs are finite; a program needn't handle non-finite values.
Results may differ from the reference program's by a relative error of at most 0.0023.
Values may be sent and summed in bfloat16 or wider, within the bound.
A program may use at most 320 MiB of HBM per device.

```python
import jax
import jax.numpy as jnp
from jax import lax

N = 12288
BLK = 128
HOT = 2
NPAIR = 64
NHB = 48
NTILE = 8
BT = 12


def draw_start_vector(key, part):
    base = jax.random.normal(key, (N, N), jnp.float32)
    return jnp.clip((base + base.T) * 0.7071067811865476, -6.0, 6.0)


def draw_pair_lists(key, part):
    key_source, key_target, key_ham = jax.random.split(jax.random.fold_in(key, 11), 3)
    pair_shape = (NTILE, NPAIR)
    random_source = jax.random.randint(key_source, pair_shape, 0, NTILE)
    position = jnp.arange(NPAIR, dtype=jnp.int32)[None, :] + jnp.zeros((NTILE, 1), jnp.int32)
    source = jnp.where(position < NTILE, position, random_source)
    target = jax.random.randint(key_target, pair_shape, 0, BT)
    ham_ids = jax.random.randint(key_ham, pair_shape, 0, NHB)
    return jnp.stack([source, target, ham_ids]).astype(jnp.int32)


def draw_pair_counts(key, part):
    lowest = max(NTILE, NPAIR // 4)
    spread_size = NPAIR - lowest
    first_key, second_key, third_key = jax.random.split(jax.random.fold_in(key, 13), 3)
    first_draw = jax.random.randint(first_key, (NTILE,), 0, spread_size + 1)
    second_draw = jax.random.randint(second_key, (NTILE,), 0, spread_size + 1)
    drawn = lowest + first_draw * second_draw // max(spread_size, 1)
    busiest = jax.random.randint(third_key, (), 0, NTILE)
    return jnp.where(jnp.arange(NTILE) == busiest, NPAIR, drawn).astype(jnp.int32)


def draw_hot_blocks(key, part):
    scores = jax.random.randint(jax.random.fold_in(key, 17), (NTILE, BT), 0, 1 << 20) * BT + jnp.arange(BT, dtype=jnp.int32)[None, :]
    ordering = jnp.argsort(scores, axis=1)
    return ordering[:, :HOT].astype(jnp.int32)


def plant(result, stream_key, low, largest):
    longest = result.shape.index(max(result.shape))
    spots = []
    for shift in (0, 1):
        where = [jax.random.randint(jax.random.fold_in(stream_key, axis), (), 0, length) for axis, length in enumerate(result.shape)]
        where[longest] = (where[longest] + shift) % result.shape[longest]
        spots.append(tuple(where))
    return result.at[spots[0]].set(low).at[spots[1]].set(largest)


def block_scale(stream_key, shape, cuts, low, largest):
    loudness = 1.0
    for axis_at, blocks in cuts:
        heights = jax.random.uniform(jax.random.fold_in(jax.random.fold_in(stream_key, 6), axis_at), (blocks,), jnp.float32, low / len(cuts), largest / len(cuts))
        loudness = loudness * jnp.repeat(jnp.exp(heights), shape[axis_at] // blocks).reshape((-1,) + (1,) * (len(shape) - 1 - axis_at))
    return loudness


def centred(key, dims, deviation, most, cuts=(), kind=jnp.bfloat16):
    array = deviation * jax.random.normal(key, dims, jnp.float32)
    if cuts:
        array = array * block_scale(key, dims, cuts, -0.22, 0.18)
    return jnp.clip(array, -most, most).astype(kind)


def setup_inputs(seed: int = 0) -> dict:
    seeds = jax.random.split(jax.random.key(seed), 8)
    return {
        "start_vector": draw_start_vector(jax.random.fold_in(seeds[7], 71), 0),
        "ham_blocks": centred(seeds[1], (NTILE * NHB, BLK, BLK), (BLK * 8) ** -0.5, 0.1875, ((0, 8),)),
        "diagonal": jnp.clip(jax.random.uniform(seeds[2], (N,), jnp.float32, -1.0, 1.0), -1.0, 1.0),
        "pair_lists": draw_pair_lists(jax.random.fold_in(seeds[7], 71), 0),
        "pair_counts": draw_pair_counts(jax.random.fold_in(seeds[7], 71), 0),
        "hot_blocks": draw_hot_blocks(jax.random.fold_in(seeds[7], 71), 0),
        "selection": plant(jax.random.randint(seeds[6], (NTILE, NTILE), 0, HOT), jax.random.fold_in(seeds[6], 1), 0, HOT - 1).astype(jnp.int32),
    }


center = 0.25
half_width = 2.5


def operator(iterate, ham_blocks, diagonal, pair_lists, pair_counts, hot_blocks, selection):
    tile_rows = N // NTILE
    rounded = lax.optimization_barrier(iterate.astype(jnp.bfloat16)).astype(jnp.float32)
    ham_wide = ham_blocks.astype(jnp.float32)

    def update(flat_index, accumulated):
        target_tile = flat_index // NPAIR
        pair_index = flat_index % NPAIR
        source_tile = pair_lists[0, target_tile, pair_index]
        target_block = pair_lists[1, target_tile, pair_index]
        block_id = pair_lists[2, target_tile, pair_index]
        chosen = hot_blocks[source_tile, selection[target_tile, source_tile]]
        src_start = (source_tile * tile_rows + chosen * BLK).astype(jnp.int32)
        source = lax.dynamic_slice_in_dim(rounded, src_start, BLK, 0)
        ham_block = lax.dynamic_index_in_dim(ham_wide, (target_tile * NHB + block_id).astype(jnp.int32), 0, keepdims=False)
        product = jnp.dot(ham_block, source, preferred_element_type=jnp.float32)
        is_live = (pair_index < pair_counts[target_tile]).astype(jnp.float32)
        row_start = (target_tile * tile_rows + target_block * BLK).astype(jnp.int32)
        current = lax.dynamic_slice_in_dim(accumulated, row_start, BLK, 0)
        return lax.dynamic_update_slice_in_dim(accumulated, current + is_live * product, row_start, 0)

    one_side = lax.fori_loop(0, NTILE * NPAIR, update, jnp.zeros((N, N), jnp.float32))
    return one_side + one_side.T + (diagonal[:, None] + diagonal[None, :]) * iterate


def reference(start_vector, ham_blocks, diagonal, pair_lists, pair_counts, hot_blocks, selection):
    first_iterate = (operator(start_vector, ham_blocks, diagonal, pair_lists, pair_counts, hot_blocks, selection) - center * start_vector) / half_width
    second_iterate = 2.0 * (operator(first_iterate, ham_blocks, diagonal, pair_lists, pair_counts, hot_blocks, selection) - center * first_iterate) / half_width - start_vector
    return first_iterate, second_iterate
```

```python
import functools

import jax
import jax.numpy as jnp
from jax import lax
from jax.experimental import pallas as pl
from jax.experimental.pallas import tpu as pltpu
from jax.sharding import PartitionSpec as P

center = 0.25
half_width = 2.5
VMEM_LIMIT = 60 * 1024 * 1024


def dense_kernel(transposed, tiles, pairs, counts, ham_ref, out_ref, acc):
    tile = tiles[pl.program_id(0)]
    tile_count = counts.shape[0]
    slots = pairs.shape[0] // (3 * tile_count)
    size = ham_ref.shape[-1]
    acc[...] = jnp.zeros_like(acc)

    def add(slot, carry):
        at = tile * slots + slot
        source = pl.multiple_of(pairs[at] * size, size)
        target = pl.multiple_of(pairs[tile_count * slots + at] * size, size)
        block = ham_ref[0, pairs[2 * tile_count * slots + at]].astype(jnp.float32)
        if transposed:
            acc[pl.ds(source, size), pl.ds(target, size)] += block.T
        else:
            acc[pl.ds(target, size), pl.ds(source, size)] += block
        return carry

    lax.fori_loop(0, counts[tile], add, 0)
    out_ref[0] = acc[...].astype(out_ref.dtype)


def dense(hams, tiles, pairs, counts, shape, transposed):
    grid_spec = pltpu.PrefetchScalarGridSpec(
        num_scalar_prefetch=3,
        grid=(hams.shape[0],),
        in_specs=[pl.BlockSpec((1,) + hams.shape[1:], lambda i, *_: (i, 0, 0, 0))],
        out_specs=pl.BlockSpec((1,) + shape, lambda i, *_: (i, 0, 0)),
        scratch_shapes=[pltpu.VMEM(shape, jnp.float32)],
    )
    return pl.pallas_call(
        functools.partial(dense_kernel, transposed),
        out_shape=jax.ShapeDtypeStruct((hams.shape[0],) + shape, jnp.bfloat16),
        grid_spec=grid_spec,
        compiler_params=pltpu.CompilerParams(vmem_limit_bytes=VMEM_LIMIT),
    )(tiles, pairs, counts, hams)


def round_kernel(place, hot, sel, x_ref, out_ref):
    out_ref[0] = x_ref[...].astype(out_ref.dtype)


def gather_rows(x, place, hot, sel, row_count, size):
    width = x.shape[1]
    hot_count = hot.shape[0] // row_count

    def pick(p, place, hot, sel):
        p = jnp.minimum(p, row_count - 1)
        return (hot[place[0] * hot_count + sel[p * row_count + place[0]]], 0)

    grid_spec = pltpu.PrefetchScalarGridSpec(
        num_scalar_prefetch=3,
        grid=(row_count,),
        in_specs=[pl.BlockSpec((size, width), pick)],
        out_specs=pl.BlockSpec((1, size, width), lambda p, *_: (p, 0, 0)),
    )
    return pl.pallas_call(
        round_kernel,
        out_shape=jax.ShapeDtypeStruct((row_count, size, width), jnp.bfloat16),
        grid_spec=grid_spec,
    )(place, hot, sel, x)


def gather_cols(x, place, hot, sel, row_count, ratio, size):
    height = x.shape[0]
    hot_count = hot.shape[0] // row_count
    blocks = x.shape[1] // (ratio * size)

    def pick(n, place, hot, sel):
        n = jnp.minimum(n, ratio * hot_count - 1)
        tile, which = n // hot_count, n % hot_count
        return (0, tile * blocks + hot[(place[1] * ratio + tile) * hot_count + which])

    grid_spec = pltpu.PrefetchScalarGridSpec(
        num_scalar_prefetch=3,
        grid=(ratio * hot_count,),
        in_specs=[pl.BlockSpec((height, size), pick)],
        out_specs=pl.BlockSpec((1, height, size), lambda n, *_: (n, 0, 0)),
    )
    return pl.pallas_call(
        round_kernel,
        out_shape=jax.ShapeDtypeStruct((ratio * hot_count, height, size), jnp.bfloat16),
        grid_spec=grid_spec,
    )(place, hot, sel, x)


def spread_hams(ham, row_n, col_n):
    ratio = row_n // col_n
    side = lax.rem(lax.axis_index("row"), ratio)
    group = lax.axis_index("row") // ratio
    dist = lax.rem(group - lax.axis_index("col") + col_n, col_n)
    bwd = (col_n - 1) // 2
    fwd = col_n - 1 - bwd

    def device(group, side, col):
        return ((group % col_n) * ratio + side) * col_n + col

    held = ham
    for way, count in ((1, fwd), (-1, bwd)):
        moving = ham
        for step in range(count):
            links = [(device(col + way * step, s, col), device(col + way * (step + 1), s, col))
                     for col in range(col_n) for s in range(ratio)]
            moving = lax.ppermute(moving, ("row", "col"), links)
            held = jnp.where(dist == (way * (step + 1)) % col_n, moving, held)
    pieces = [held]
    for m in range(1, ratio):
        links = [(device(g, s, col), device(g, (s + m) % ratio, col))
                 for g in range(col_n) for col in range(col_n) for s in range(ratio)]
        pieces.append(lax.ppermute(held, ("row", "col"), links))
    order = lax.rem(side - jnp.arange(ratio) + ratio, ratio)
    return jnp.take(jnp.stack(pieces), order, axis=0)


def exchange(rows_in, cols_in):
    rows = lax.all_to_all(rows_in, "row", split_axis=0, concat_axis=0, tiled=True)
    return rows, lax.all_gather(cols_in, "col")


def filter_kernel(source_count, row_chunk, last, place, sel, wa_ref, s_ref, wb_ref, rd_ref, cd_ref, *refs):
    b_refs = refs[:source_count]
    rest = refs[source_count:]
    if last:
        x_ref, start_ref, out_ref = rest
    else:
        x_ref, out_ref = rest

    def chunk(i, carry):
        rows = pl.ds(pl.multiple_of(i * row_chunk, row_chunk), row_chunk)
        beta = jnp.concatenate([b[0, rows, :] for b in b_refs], axis=1)
        acc = jnp.dot(wa_ref[rows, :], s_ref[...], preferred_element_type=jnp.float32)
        acc = acc + jnp.dot(beta, wb_ref[0], preferred_element_type=jnp.float32)
        x = x_ref[rows, :]
        acc = acc + (rd_ref[rows, :] + cd_ref[...] - center) * x
        if last:
            out_ref[rows, :] = acc * (2.0 / half_width) - start_ref[rows, :]
        else:
            out_ref[rows, :] = acc * (1.0 / half_width)
        return carry

    lax.fori_loop(0, x_ref.shape[0] // row_chunk, chunk, 0)


def filter_step(place, sel, wa, s, wb, rd, cd, cols, x, start, row_n, ratio):
    height, width = x.shape
    size = cols.shape[-1]
    hot_count = cols.shape[0] // row_n
    tile_width = width // ratio
    stripe = 256 if tile_width % 256 == 0 else size
    per_tile = tile_width // stripe
    row_chunk = height // 3 if height % 384 == 0 else size
    last = start is not None

    def b_spec(q):
        return pl.BlockSpec(
            (1, height, size),
            lambda n, place, sel: (q * hot_count + sel[(place[1] * ratio + jnp.minimum(n // per_tile, ratio - 1)) * row_n + q], 0, 0))

    striped = pl.BlockSpec((height, stripe), lambda n, *_: (0, n))
    in_specs = [
        pl.BlockSpec(wa.shape, lambda n, *_: (0, 0)),
        pl.BlockSpec((s.shape[0], stripe), lambda n, *_: (0, n)),
        pl.BlockSpec((1, wb.shape[1], stripe), lambda n, *_: (n // per_tile, 0, n % per_tile)),
        pl.BlockSpec((height, 1), lambda n, *_: (0, 0)),
        pl.BlockSpec((1, stripe), lambda n, *_: (0, n)),
    ] + [b_spec(q) for q in range(row_n)] + [striped] * (2 if last else 1)
    args = [wa, s, wb, rd, cd] + [cols] * row_n + [x] + ([start] if last else [])
    grid_spec = pltpu.PrefetchScalarGridSpec(
        num_scalar_prefetch=2, grid=(width // stripe,), in_specs=in_specs, out_specs=striped)
    return pl.pallas_call(
        functools.partial(filter_kernel, row_n, row_chunk, last),
        out_shape=jax.ShapeDtypeStruct(x.shape, jnp.float32),
        grid_spec=grid_spec,
        compiler_params=pltpu.CompilerParams(vmem_limit_bytes=VMEM_LIMIT),
    )(place, sel, *args)


def body(start_vector, ham_blocks, diagonal, pair_lists, pair_counts, hot_blocks, selection):
    row_n = lax.axis_size("row")
    col_n = lax.axis_size("col")
    ratio = row_n // col_n
    height, width = start_vector.shape
    size = ham_blocks.shape[1]
    row_index = lax.axis_index("row")
    col_index = lax.axis_index("col")
    place = jnp.stack([row_index, col_index]).astype(jnp.int32)
    pairs = pair_lists.reshape(-1)
    hot = hot_blocks.reshape(-1)
    sel = selection.reshape(-1)
    rd = lax.dynamic_slice_in_dim(diagonal, row_index * height, height)[:, None]
    cd = lax.dynamic_slice_in_dim(diagonal, col_index * width, width)[None, :]
    depth = row_n * size

    def sources(x):
        rows = gather_rows(x, place, hot, sel, row_n, size)
        cols = gather_cols(x, place, hot, sel, row_n, ratio, size)
        return rows, cols

    def joined(rows, cols):
        return rows.reshape(depth, width), cols.reshape((-1,) + cols.shape[2:])

    rows, cols = exchange(*sources(start_vector))
    hams = spread_hams(ham_blocks, row_n, col_n)
    wa = dense(ham_blocks[None], place[:1], pairs, pair_counts, (height, depth), False)[0]
    mirrors = (col_index * ratio + jnp.arange(ratio)).astype(jnp.int32)
    wb = dense(hams, mirrors, pairs, pair_counts, (depth, width // ratio), True)
    s, b = joined(rows, cols)
    first = filter_step(place, sel, wa, s, wb, rd, cd, b, start_vector, None, row_n, ratio)
    s, b = joined(*exchange(*sources(first)))
    second = filter_step(place, sel, wa, s, wb, rd, cd, b, first, start_vector, row_n, ratio)
    return (first, second)


def solution(mesh):
    in_specs = (P("row", "col"), P("row", None, None), P(), P(), P(), P(), P())
    out_specs = (P("row", "col"), P("row", "col"))
    return jax.shard_map(body, mesh=mesh, in_specs=in_specs, out_specs=out_specs, check_vma=False)
```
